32 devices in a mesh: blk: 4 (over y, x), grp: 8 (over z, core).
Axes of the slice: x: 2, y: 2, z: 4, core: 2. Of those that a mesh axis runs over, the one named last changes fastest.
Arguments:
- h_blocks: bfloat16 [1536, 16, 128, 128], P(('blk', 'grp')), may hold values from -0.0625 to 0.0625
- h_cols: int32 [1536, 16], P(('blk', 'grp')), may hold values from 0 to 1535, as said below
- t_prev: bfloat16 [196608, 128], P(('blk', 'grp')), may hold values from -6 to 6
- t_cur: bfloat16 [196608, 128], P(('blk', 'grp')), may hold values from -6 to 6
- cheb_coeffs: float32 [3], replicated, may hold values from 0.4 to 1
- owner_slot: int32 [128], replicated, may hold values from 0 to 127, each once
Outputs:
- t_next: bfloat16 [196608, 128], P(('blk', 'grp'))
- t_last: bfloat16 [196608, 128], P(('blk', 'grp'))
- owner_density: float32 [128, 196608], P(('blk', 'grp'))
The draws below stay inside these ranges and needn't reach their ends.
Inputs may be any that keep to these rules, and one draw needn't show every extreme that they name: Block column h_cols[i, k] lies within 24 block rows of i, counted around the ends (periodically); distances of exactly 24 occur both ways; a name may repeat within a row. `owner_slot`: each row of the owner layout receives exactly one window column.
All inputs are finite; a program needn't handle non-finite values.
Results may differ from the reference program's by a relative error of at most 0.009.
Values may be sent and summed in bfloat16 or wider, within the bound.
A program may use at most 192 MiB of HBM per device.

```python
import jax
import jax.numpy as jnp
from jax import lax

BS = 128
NBLK = 1536
KNZ = 16
COLS = 128
ORDER = 196608
REACH = 24


def draw_h_cols(key, part):
    offsets = jax.random.randint(key, (NBLK, KNZ), -REACH, REACH + 1)
    offsets = offsets.at[0, 0].set(-1).at[0, 1].set(REACH).at[0, 2].set(-REACH).at[1, 0].set(-1)
    rows = jnp.arange(NBLK, dtype=jnp.int32)[:, None]
    return ((rows + offsets) % NBLK).astype(jnp.int32)


def shard_levels(key, extent, cuts, low, high):
    gain, own = 1.0, jax.random.fold_in(key, 6)
    for position, shards_of in cuts:
        heights = jnp.exp(jax.random.uniform(jax.random.fold_in(own, position), (shards_of,), jnp.float32, low / len(cuts), high / len(cuts)))
        gain = gain * jnp.repeat(heights, extent[position] // shards_of).reshape([-1 if axis == position else 1 for axis in range(len(extent))])
    return gain


def bell_draw(own_key, shape, scale, reach, pieces=(), kind=jnp.bfloat16):
    loudness = shard_levels(own_key, shape, pieces, -0.22, 0.18) if pieces else 1.0
    result = jax.random.normal(own_key, shape, jnp.float32) * scale * loudness
    return jnp.minimum(jnp.maximum(result, -reach), reach).astype(kind)


def setup_inputs(seed: int = 0) -> dict:
    streams_of = jax.random.split(jax.random.key(seed), 7)
    return {
        "h_blocks": bell_draw(streams_of[0], (NBLK, KNZ, BS, BS), (4 * KNZ * BS) ** -0.5, 0.0625, ((0, 32),)),
        "h_cols": draw_h_cols(jax.random.fold_in(streams_of[6], 71), 0),
        "t_prev": bell_draw(streams_of[2], (ORDER, COLS), 1.0, 6.0, ((0, 32),)),
        "t_cur": bell_draw(streams_of[3], (ORDER, COLS), 1.0, 6.0, ((0, 32),)),
        "cheb_coeffs": jnp.clip(jax.random.uniform(streams_of[4], (3,), jnp.float32, 0.4, 1.0), 0.4, 1.0),
        "owner_slot": jax.random.permutation(streams_of[5], COLS).astype(jnp.int32),
    }


def apply_h(h_blocks, h_cols, current):
    blocks = current.reshape(NBLK, BS, COLS)

    def one_slot(total, slot):
        picked = jnp.take(blocks, jnp.take(h_cols, slot, axis=1), axis=0).astype(jnp.float32)
        tile = jnp.take(h_blocks, slot, axis=1).astype(jnp.float32)
        return total + jnp.einsum('iab,ibm->iam', tile, picked), None

    total, unused = lax.scan(one_slot, jnp.zeros((NBLK, BS, COLS), jnp.float32), jnp.arange(KNZ, dtype=jnp.int32))
    return total.reshape(NBLK * BS, COLS)


def reference(h_blocks, h_cols, t_prev, t_cur, cheb_coeffs, owner_slot):
    before, current = t_prev, t_cur
    made = []
    for term in range(3):
        fresh = (2.0 * apply_h(h_blocks, h_cols, current) - before.astype(jnp.float32)).astype(jnp.bfloat16)
        made.append(fresh)
        before, current = current, fresh
    density = cheb_coeffs[0] * made[0].astype(jnp.float32)
    density = density + cheb_coeffs[1] * made[1].astype(jnp.float32)
    density = density + cheb_coeffs[2] * made[2].astype(jnp.float32)
    owner_density = jnp.zeros((COLS, NBLK * BS), jnp.float32).at[owner_slot].set(density.T)
    return made[1], made[2], owner_density
```

```python
import functools

import jax
import jax.numpy as jnp
from jax import lax
from jax.experimental import pallas as pl
from jax.experimental.pallas import tpu as pltpu
from jax.sharding import PartitionSpec as P

AXES = ("blk", "grp")

MESH = pl.DeviceIdType.MESH


def hops_of(devices):
    hops, known = [], 1
    while known < devices // 2:
        hops.append(known)
        known *= 2
    return hops


def row_product(cols, row, h_ref, ext, cut):
    slots, last = h_ref.shape[1], ext.shape[0] - 1
    at = [cols[row, k] if cut == 0 else jnp.clip(cols[row, k] - cut, 0, last) for k in range(slots)]
    rhs = jnp.concatenate([ext[a] for a in at], axis=0)
    lhs = jnp.concatenate([h_ref[row, k] for k in range(slots)], axis=1)
    return jnp.dot(lhs, rhs, preferred_element_type=jnp.float32)


def whole_kernel(
    shape, h_cols, coeffs, owner, h_hbm, prev_hbm, cur_hbm, next_out, last_out, arrived,
    h_ref, ext_a, ext_b, ext_c, near_a, near_c, prev_ref, last_ref, packed, stage, chooser, cols,
    load_sem, h_sem, send_sem, recv_sem, move_sem, spread_sem, gather_sem, out_sem, meet_sem,
):
    reach, pieces, per_dev, group = shape
    rows, _, bs, width = h_ref.shape[0], h_ref.shape[1], h_ref.shape[2], ext_a.shape[2]
    piece = reach // pieces
    blks, grps = lax.axis_size("blk"), lax.axis_size("grp")
    devices = blks * grps
    blk, grp = lax.axis_index("blk"), lax.axis_index("grp")
    me = blk * grps + grp

    def place(linear):
        return (linear // grps, linear % grps)

    half = pieces // 2
    inner = half * piece
    first_side = grp % 2

    def middle_first(c):
        side = (first_side + c // half) % 2
        edge = c // pieces
        return side, edge, side * reach + spot(side, edge, c % half)

    def edge_first(c):
        side = (first_side + c // pieces) % 2
        edge = 1 - (c // half) % 2
        return side, edge, side * reach + spot(side, edge, c % half)

    def spot(side, edge, j):
        return ((edge + side + 1) % 2) * inner + j * piece

    def h_load(c):
        base = middle_first(c)[2]
        where = pl.ds(base, piece)
        return pltpu.make_async_copy(h_hbm.at[where], h_ref.at[where], h_sem.at[c])

    def halo(term, source, offset, full, near, where):
        side, edge, base = where
        there = (1 - 2 * side) * rows + base + reach
        if near is None:
            dest = full.at[pl.ds(there, piece)]
        else:
            dest = near.at[pl.ds(there - inner, piece)]
        slot = (base - side * reach) // piece
        return pltpu.make_async_remote_copy(
            src_ref=source.at[pl.ds(offset + base, piece)],
            dst_ref=dest,
            send_sem=send_sem.at[term, side, slot],
            recv_sem=recv_sem.at[term, side, slot],
            device_id=place((me + devices - 1 + 2 * side) % devices),
            device_id_type=MESH,
        )

    prev_load = pltpu.make_async_copy(prev_hbm, prev_ref, load_sem.at[0])
    cur_load = pltpu.make_async_copy(cur_hbm, ext_a.at[pl.ds(reach, rows)], load_sem.at[1])
    near_load = pltpu.make_async_copy(cur_hbm, near_a.at[pl.ds(inner, rows)], load_sem.at[2])
    barrier = pltpu.get_barrier_semaphore()

    def signal_pair(semaphore, hop):
        for other in (me + hop, me + devices - hop):
            pl.semaphore_signal(semaphore, inc=1, device_id=place(other % devices), device_id_type=MESH)

    signal_pair(barrier, 1)
    cur_load.start()
    near_load.start()
    prev_load.start()
    pl.semaphore_wait(barrier, 2)
    start_order = [edge_first(c) for c in range(2 * pieces)]
    edges = [c for c in range(2 * pieces) if (c // half) % 2 == 0]
    outers = [c for c in range(2 * pieces) if (c // half) % 2 == 1]
    for c in edges:
        halo(0, cur_hbm, 0, ext_a, near_a, start_order[c]).start()
    cur_load.wait()
    for c in outers:
        halo(0, ext_a, reach, ext_a, None, start_order[c]).start()
    for c in range(pieces):
        h_load(c).start()

    hops = hops_of(devices)

    ahead = list(range(len(hops) + 1))

    def meet():
        if ahead:
            step = ahead.pop(0)
            if step > 0:
                pl.semaphore_wait(meet_sem.at[step - 1], 2)
            if step < len(hops):
                signal_pair(meet_sem.at[step], hops[step])

    meet()

    q = lax.broadcasted_iota(jnp.int32, chooser.shape, 0)
    slot = (q % devices) * per_dev + q // devices
    chooser[...] = jnp.where(slot == owner[...], 1.0, 0.0).astype(chooser.dtype)

    total_rows = rows * devices

    def local_row(row, carry):
        for k in range(h_ref.shape[1]):
            at = h_cols[k, row] - me * rows + reach
            at = jnp.where(at < 0, at + total_rows, at)
            at = jnp.where(at >= total_rows, at - total_rows, at)
            cols[row, k] = jnp.clip(at, 0, rows + 2 * reach - 1)
        return carry

    lax.fori_loop(0, rows, local_row, 0)
    for c in range(pieces, 2 * pieces):
        h_load(c).start()
    meet()
    prev_load.wait()
    near_load.wait()

    def rows_of(where, ext, cut, old, old_at, stores):
        for r in range(piece):
            row = where[2] + r
            total = row_product(cols, row, h_ref, ext, cut)
            fresh = 2.0 * total - old[old_at + row].astype(jnp.float32)
            for new, new_at in stores:
                new[new_at + row] = fresh.astype(new.dtype)

    def loop(low, high, order, ext, cut, old, old_at, stores, ready, done):
        def one_piece(c, carry):
            where = order(c)
            ready(c)
            rows_of(where, ext, cut, old, old_at, stores)
            done(c, where)
            return carry

        lax.fori_loop(low, high, one_piece, 0)

    def split_term(term, source, offset, ext, near, old, old_at, stores, ready, done):
        for c in edges:
            halo(term, source, offset, ext, near, start_order[c]).wait()
        meet()
        moves = [
            pltpu.make_async_copy(near.at[pl.ds(0, inner)], ext.at[pl.ds(inner, inner)], move_sem.at[0]),
            pltpu.make_async_copy(
                near.at[pl.ds(inner + rows, inner)], ext.at[pl.ds(reach + rows, inner)], move_sem.at[1]
            ),
        ]
        for m in moves:
            m.start()
        loop(0, pieces, middle_first, near, inner, old, old_at, stores, ready, done)
        for m in moves:
            m.wait()
        for c in outers:
            halo(term, source, offset, ext, None, start_order[c]).wait()
        meet()
        loop(pieces, 2 * pieces, middle_first, ext, 0, old, old_at, stores, ready, done)

    def nothing(c):
        pass

    split_term(
        0, ext_a, reach, ext_a, near_a, prev_ref, 0, [(ext_b, reach)],
        lambda c: h_load(c).wait(),
        lambda c, where: halo(1, ext_b, reach, ext_b, None, where).start(),
    )
    meet()
    for c in range(2 * pieces):
        halo(1, ext_b, reach, ext_b, None, start_order[c]).wait()
    both = [(ext_c, reach), (near_c, inner)]
    for part in range(4):
        to_near = near_c if part % 2 == 0 else None
        meet()
        loop(
            part * half, (part + 1) * half, edge_first, ext_b, 0, ext_a, reach, both, nothing,
            lambda c, where: halo(2, ext_c, reach, ext_c, to_near, where).start(),
        )
    while ahead:
        meet()
    next_store = pltpu.make_async_copy(ext_c.at[pl.ds(reach, rows)], next_out, out_sem.at[0])
    next_store.start()

    def pack(first):
        for b in range(group):
            row = first + b
            dens = coeffs[0] * ext_b[reach + row].astype(jnp.float32)
            dens = dens + coeffs[1] * ext_c[reach + row].astype(jnp.float32)
            dens = dens + coeffs[2] * last_ref[row].astype(jnp.float32)
            turned = lax.dot_general(
                chooser[...], dens.astype(jnp.bfloat16), (((1,), (1,)), ((), ())),
                preferred_element_type=jnp.float32,
            )
            for s in range(per_dev):
                stage[pl.ds(b * per_dev + s, devices, stride=group * per_dev), :] = turned[
                    s * devices : (s + 1) * devices
                ]
        span = group * per_dev
        tiles = stage[...].reshape(devices, span, bs).astype(packed.dtype)
        packed[:, pl.ds(pl.multiple_of(first * per_dev, span), span), :] = tiles

    def spread(base, count):
        where = pl.ds(base * per_dev, count * per_dev)

        def one(i, carry):
            k = i // blks
            turn = (grps // 2 + (1 - 2 * (k % 2)) * ((k + 1) // 2) + grps) % grps
            to_blk = (blk + i + 1) % blks
            to_grp = (grp + turn) % grps
            pltpu.make_async_remote_copy(
                src_ref=packed.at[to_blk * grps + to_grp, where],
                dst_ref=arrived.at[me, where],
                send_sem=spread_sem,
                recv_sem=gather_sem,
                device_id=(to_blk, to_grp),
                device_id_type=MESH,
            ).start()
            return carry

        lax.fori_loop(0, devices - 1, one, 0)

    interleaved = piece % group == 0

    def last_done(c, where):
        if interleaved:
            base = where[2]

            def one_group(g, carry):
                pack(base + g * group)
                return carry

            lax.fori_loop(0, piece // group, one_group, 0)

            @pl.when(c == pieces - 1)
            def _():
                spread(inner, reach)

            @pl.when((c >= pieces) & (c % half == half - 1))
            def _():
                spread(base - (half - 1) * piece, half * piece)

    split_term(2, ext_c, reach, ext_c, near_c, ext_b, reach, [(last_ref, 0)], nothing, last_done)
    last_store = pltpu.make_async_copy(last_ref, last_out, out_sem.at[1])
    last_store.start()
    if not interleaved:
        for g in range(rows // group):
            pack(g * group)
        spread(0, rows)
    own = pltpu.make_async_copy(packed.at[me], arrived.at[me], out_sem.at[2])
    own.start()
    everything = pltpu.make_async_remote_copy(
        src_ref=packed.at[pl.ds(0, devices - 1)],
        dst_ref=arrived.at[pl.ds(0, devices - 1)],
        send_sem=spread_sem,
        recv_sem=gather_sem,
        device_id=place((me + 1) % devices),
        device_id_type=MESH,
    )
    everything.wait()
    own.wait()
    next_store.wait()
    last_store.wait()


def in_hbm(array):
    return pltpu.with_memory_space_constraint(array, pltpu.HBM)


def finish_kernel(steps, next_ref, last_ref, arrived, next_out, last_out, owned, wide, sems):
    copies = [
        pltpu.make_async_copy(next_ref, next_out, sems.at[0]),
        pltpu.make_async_copy(last_ref, last_out, sems.at[1]),
    ]
    for c in copies:
        c.start()
    step = arrived.shape[0] // steps
    for i in range(steps):
        where = pl.ds(i * step, step)
        wide[where] = arrived[where].astype(wide.dtype)
        c = pltpu.make_async_copy(wide.at[where], owned.at[where], sems.at[2 + i])
        c.start()
        copies.append(c)
    for c in copies:
        c.wait()


def finish(made_next, made_last, arrived):
    steps = 4
    anyspec = pl.BlockSpec(memory_space=pl.ANY)
    vmem = pl.BlockSpec(memory_space=pltpu.VMEM)
    term = jax.ShapeDtypeStruct(made_next.shape, made_next.dtype)
    return pl.pallas_call(
        functools.partial(finish_kernel, steps),
        out_shape=(term, term, jax.ShapeDtypeStruct(arrived.shape, jnp.float32)),
        in_specs=[anyspec, anyspec, vmem],
        out_specs=(anyspec, anyspec, anyspec),
        scratch_shapes=[
            pltpu.VMEM(arrived.shape, jnp.float32),
            pltpu.SemaphoreType.DMA((2 + steps,)),
        ],
        compiler_params=pltpu.CompilerParams(vmem_limit_bytes=16 * 1024 * 1024),
        name="finish",
    )(made_next, made_last, arrived)


def on_device(h_blocks, h_cols, t_prev, t_cur, cheb_coeffs, owner_slot):
    rows, slots, bs, _ = h_blocks.shape
    width = t_cur.shape[1]
    devices = lax.axis_size(AXES)
    reach = rows // 2
    per_dev = width // devices
    pieces = next(p for p in (6, 2) if reach % p == 0)
    group = max(1, 16 // per_dev)
    group = group if rows % group == 0 else rows
    anyspec = pl.BlockSpec(memory_space=pl.ANY)
    hbm = pl.BlockSpec(memory_space=pltpu.HBM)
    smem = pl.BlockSpec(memory_space=pltpu.SMEM)
    vmem = pl.BlockSpec(memory_space=pltpu.VMEM)
    dma = pltpu.SemaphoreType.DMA
    term = jax.ShapeDtypeStruct((rows, bs, width), t_cur.dtype)
    ext = pltpu.VMEM((rows + 2 * reach, bs, width), t_cur.dtype)
    near = pltpu.VMEM((rows + reach, bs, width), t_cur.dtype)
    own = pltpu.VMEM((rows, bs, width), t_cur.dtype)
    made_next, made_last, arrived = pl.pallas_call(
        functools.partial(whole_kernel, (reach, pieces, per_dev, group)),
        out_shape=(term, term, jax.ShapeDtypeStruct((devices, rows * per_dev, bs), jnp.bfloat16)),
        in_specs=[smem, smem, vmem, hbm, hbm, hbm],
        out_specs=(anyspec, anyspec, anyspec),
        scratch_shapes=[
            pltpu.VMEM(h_blocks.shape, h_blocks.dtype),
            ext,
            ext,
            ext,
            near,
            near,
            own,
            own,
            pltpu.VMEM((devices, rows * per_dev, bs), jnp.bfloat16),
            pltpu.VMEM((devices * group * per_dev, bs), jnp.float32),
            pltpu.VMEM((width, width), jnp.bfloat16),
            pltpu.SMEM((rows, slots), jnp.int32),
            dma((3,)),
            dma((2 * pieces,)),
            dma((3, 2, pieces)),
            dma((3, 2, pieces)),
            dma((2,)),
            dma,
            dma,
            dma((3,)),
            pltpu.SemaphoreType.REGULAR((len(hops_of(devices)),)),
        ],
        compiler_params=pltpu.CompilerParams(collective_id=0, has_side_effects=True, vmem_limit_bytes=46 * 1024 * 1024),
        name="whole",
    )(
        in_hbm(h_cols.T),
        in_hbm(cheb_coeffs),
        in_hbm(owner_slot[None, :]),
        h_blocks,
        in_hbm(t_prev.reshape(rows, bs, width)),
        in_hbm(t_cur.reshape(rows, bs, width)),
    )
    made_next, made_last, owned = finish(made_next, made_last, arrived)
    owned = owned.reshape(devices * rows, per_dev, bs)
    owned = owned.transpose(1, 0, 2).reshape(per_dev, devices * rows * bs)
    return (made_next.reshape(-1, width), made_last.reshape(-1, width), owned)


def solution(mesh):
    return jax.shard_map(
        on_device,
        mesh=mesh,
        in_specs=(
            P(("blk", "grp"), None, None, None),
            P(("blk", "grp"), None),
            P(("blk", "grp"), None),
            P(("blk", "grp"), None),
            P(),
            P(),
        ),
        out_specs=(P(("blk", "grp"), None), P(("blk", "grp"), None), P(("blk", "grp"), None)),
        check_vma=False,
    )
```

```python
import functools

import jax
import jax.numpy as jnp
from jax import lax
from jax.experimental import pallas as pl
from jax.experimental.pallas import tpu as pltpu
from jax.sharding import PartitionSpec as P

AXES = ("blk", "grp")

MESH = pl.DeviceIdType.MESH


def hops_of(devices):
    hops, known = [], 1
    while known < devices // 2:
        hops.append(known)
        known *= 2
    return hops


def row_product(cols, row, h_ref, ext, cut):
    slots, last = h_ref.shape[1], ext.shape[0] - 1
    at = [cols[row, k] if cut == 0 else jnp.clip(cols[row, k] - cut, 0, last) for k in range(slots)]
    rhs = jnp.concatenate([ext[a] for a in at], axis=0)
    lhs = jnp.concatenate([h_ref[row, k] for k in range(slots)], axis=1)
    return jnp.dot(lhs, rhs, preferred_element_type=jnp.float32)


def whole_kernel(
    shape, h_cols_hbm, coeffs_hbm, owner_hbm, h_hbm, prev_hbm, cur_hbm, next_out, last_out, arrived,
    h_cols, coeffs, owner, h_ref, ext_a, ext_b, ext_c, near_a, near_c, prev_ref, last_ref, packed, stage, chooser, cols,
    load_sem, h_sem, send_sem, recv_sem, move_sem, spread_sem, gather_sem, out_sem, meet_sem, small_sem,
):
    reach, pieces, per_dev, group = shape
    rows, _, bs, width = h_ref.shape[0], h_ref.shape[1], h_ref.shape[2], ext_a.shape[2]
    piece = reach // pieces
    blks, grps = lax.axis_size("blk"), lax.axis_size("grp")
    devices = blks * grps
    blk, grp = lax.axis_index("blk"), lax.axis_index("grp")
    me = blk * grps + grp

    def place(linear):
        return (linear // grps, linear % grps)

    half = pieces // 2
    inner = half * piece
    first_side = grp % 2

    def middle_first(c):
        side = (first_side + c // half) % 2
        edge = c // pieces
        return side, edge, side * reach + spot(side, edge, c % half)

    def edge_first(c):
        side = (first_side + c // pieces) % 2
        edge = 1 - (c // half) % 2
        return side, edge, side * reach + spot(side, edge, c % half)

    def spot(side, edge, j):
        return ((edge + side + 1) % 2) * inner + j * piece

    def h_load(g):
        side = (first_side + g % 2) % 2
        where = pl.ds(side * reach + spot(side, g // 2, 0), inner)
        return pltpu.make_async_copy(h_hbm.at[where], h_ref.at[where], h_sem.at[g])

    def halo(term, source, offset, full, near, where):
        side, edge, base = where
        there = (1 - 2 * side) * rows + base + reach
        if near is None:
            dest = full.at[pl.ds(there, piece)]
        else:
            dest = near.at[pl.ds(there - inner, piece)]
        return pltpu.make_async_remote_copy(
            src_ref=source.at[pl.ds(offset + base, piece)],
            dst_ref=dest,
            send_sem=send_sem.at[term],
            recv_sem=recv_sem.at[term, side, edge],
            device_id=place((me + devices - 1 + 2 * side) % devices),
            device_id_type=MESH,
        )

    def settle(term, copied, side, edge):
        return pltpu.make_async_remote_copy(
            src_ref=copied,
            dst_ref=copied,
            send_sem=send_sem.at[term],
            recv_sem=recv_sem.at[term, side, edge],
            device_id=place((me + 1) % devices),
            device_id_type=MESH,
        )

    def landed(term, edge):
        for side in range(2):
            settle(term, ext_a.at[pl.ds(0, inner)], side, edge).wait_recv()

    jump = (grp == 0) | (grp == grps - 1)

    prev_load = pltpu.make_async_copy(prev_hbm, prev_ref, load_sem.at[0])
    cur_load = pltpu.make_async_copy(cur_hbm, ext_a.at[pl.ds(reach, rows)], load_sem.at[1])
    near_load = pltpu.make_async_copy(cur_hbm, near_a.at[pl.ds(inner, rows)], load_sem.at[2])
    barrier = pltpu.get_barrier_semaphore()

    def signal_pair(semaphore, hop):
        for other in (me + hop, me + devices - hop):
            pl.semaphore_signal(semaphore, inc=1, device_id=place(other % devices), device_id_type=MESH)

    small_loads = [
        pltpu.make_async_copy(h_cols_hbm, h_cols, small_sem.at[0]),
        pltpu.make_async_copy(coeffs_hbm, coeffs, small_sem.at[1]),
        pltpu.make_async_copy(owner_hbm, owner, small_sem.at[2]),
    ]

    def loads():
        near_load.start()
        cur_load.start()
        prev_load.start()

    signal_pair(barrier, 1)
    for c in small_loads:
        c.start()
    pl.when(jump)(loads)
    pl.semaphore_wait(barrier, 2)
    start_order = [edge_first(c) for c in range(2 * pieces)]
    edges = [c for c in range(2 * pieces) if (c // half) % 2 == 0]
    outers = [c for c in range(2 * pieces) if (c // half) % 2 == 1]
    for c in edges:
        halo(0, cur_hbm, 0, ext_a, near_a, start_order[c]).start()
    pl.when(jnp.logical_not(jump))(loads)

    def send_outers():
        for c in outers[:half]:
            halo(0, cur_hbm, 0, ext_a, None, start_order[c]).start()

    send_outers()
    for c in outers[half:]:
        halo(0, cur_hbm, 0, ext_a, None, start_order[c]).start()
    cur_load.wait()
    near_load.wait()
    prev_load.wait()
    for g in range(2):
        h_load(g).start()
    for c in small_loads:
        c.wait()
    hops = hops_of(devices)

    ahead = list(range(len(hops) + 1))

    def meet():
        if ahead:
            step = ahead.pop(0)
            if step > 0:
                pl.semaphore_wait(meet_sem.at[step - 1], 2)
            if step < len(hops):
                signal_pair(meet_sem.at[step], hops[step])

    meet()

    q = lax.broadcasted_iota(jnp.int32, chooser.shape, 0)
    slot = (q % devices) * per_dev + q // devices
    chooser[...] = jnp.where(slot == owner[...], 1.0, 0.0).astype(chooser.dtype)

    total_rows = rows * devices

    def local_row(row, carry):
        for k in range(h_ref.shape[1]):
            at = h_cols[k, row] - me * rows + reach
            at = jnp.where(at < 0, at + total_rows, at)
            at = jnp.where(at >= total_rows, at - total_rows, at)
            cols[row, k] = jnp.clip(at, 0, rows + 2 * reach - 1)
        return carry

    lax.fori_loop(0, rows, local_row, 0)
    for g in range(2, 4):
        h_load(g).start()
    meet()

    def rows_of(where, ext, cut, old, old_at, stores):
        for r in range(piece):
            row = where[2] + r
            total = row_product(cols, row, h_ref, ext, cut)
            fresh = 2.0 * total - old[old_at + row].astype(jnp.float32)
            for new, new_at in stores:
                new[new_at + row] = fresh.astype(new.dtype)

    def loop(low, high, order, ext, cut, old, old_at, stores, ready, done):
        def one_piece(c, carry):
            where = order(c)
            ready(c)
            rows_of(where, ext, cut, old, old_at, stores)
            done(c, where)
            return carry

        lax.fori_loop(low, high, one_piece, 0)

    def split_term(term, ext, near, old, old_at, stores, ready, done):
        landed(term, 1)
        moves = [
            pltpu.make_async_copy(near.at[pl.ds(0, inner)], ext.at[pl.ds(inner, inner)], move_sem.at[0]),
            pltpu.make_async_copy(
                near.at[pl.ds(inner + rows, inner)], ext.at[pl.ds(reach + rows, inner)], move_sem.at[1]
            ),
        ]
        for m in moves:
            m.start()
        while term == 2 and ahead:
            meet()
        loop(0, pieces, middle_first, near, inner, old, old_at, stores, ready, done)
        for m in moves:
            m.wait()
        landed(term, 0)
        loop(pieces, 2 * pieces, middle_first, ext, 0, old, old_at, stores, ready, done)

    def nothing(c):
        pass

    def h_ready(c):
        @pl.when(c % half == 0)
        def _():
            h_load(c // half).wait()

    split_term(
        0, ext_a, near_a, prev_ref, 0, [(ext_b, reach)], h_ready,
        lambda c, where: halo(1, ext_b, reach, ext_b, None, where).start(),
    )
    meet()
    landed(1, 1)
    landed(1, 0)
    both = [(ext_c, reach), (near_c, inner)]
    for part in range(4):
        to_near = near_c if part % 2 == 0 else None
        if part % 2 == 1:
            meet()
        loop(
            part * half, (part + 1) * half, edge_first, ext_b, 0, ext_a, reach, both, nothing,
            lambda c, where: halo(2, ext_c, reach, ext_c, to_near, where).start(),
        )
    next_store = pltpu.make_async_copy(ext_c.at[pl.ds(reach, rows)], next_out, out_sem.at[0])
    next_store.start()

    interleaved = piece % group == 0

    def place_of(row):
        return jnp.where(row < rows - inner, row + inner, row + inner - rows) if interleaved else row

    def pack(first):
        for b in range(group):
            row = first + b
            dens = coeffs[0] * ext_b[reach + row].astype(jnp.float32)
            dens = dens + coeffs[1] * ext_c[reach + row].astype(jnp.float32)
            dens = dens + coeffs[2] * last_ref[row].astype(jnp.float32)
            turned = lax.dot_general(
                chooser[...], dens.astype(jnp.bfloat16), (((1,), (1,)), ((), ())),
                preferred_element_type=jnp.float32,
            )
            for s in range(per_dev):
                stage[pl.ds(b * per_dev + s, devices, stride=group * per_dev), :] = turned[
                    s * devices : (s + 1) * devices
                ]
        span = group * per_dev
        at = place_of(first)
        tiles = stage[...].reshape(devices, span, bs).astype(packed.dtype)
        packed[:, pl.ds(pl.multiple_of(at * per_dev, span), span), :] = tiles

    def spread(base, count):
        where = pl.ds(base * per_dev, count * per_dev)

        def one(i, carry):
            k = i // blks
            turn = (grps // 2 + (1 - 2 * (k % 2)) * ((k + 1) // 2) + grps) % grps
            to_blk = (blk + i + 1) % blks
            to_grp = (grp + turn) % grps
            pltpu.make_async_remote_copy(
                src_ref=packed.at[to_blk * grps + to_grp, where],
                dst_ref=arrived.at[me, where],
                send_sem=spread_sem,
                recv_sem=gather_sem,
                device_id=(to_blk, to_grp),
                device_id_type=MESH,
            ).start()
            return carry

        lax.fori_loop(0, devices - 1, one, 0)

    def last_done(c, where):
        if interleaved:
            base = where[2]

            def one_group(g, carry):
                pack(base + g * group)
                return carry

            lax.fori_loop(0, piece // group, one_group, 0)

            @pl.when(c == pieces - 1)
            def _():
                spread(reach, reach)

            @pl.when(c == 2 * pieces - 1)
            def _():
                spread(0, reach)

    split_term(2, ext_c, near_c, ext_b, reach, [(last_ref, 0)], nothing, last_done)
    last_store = pltpu.make_async_copy(last_ref, last_out, out_sem.at[1])
    last_store.start()
    if not interleaved:
        for g in range(rows // group):
            pack(g * group)
        spread(0, rows)
    own = pltpu.make_async_copy(packed.at[me], arrived.at[me], out_sem.at[2])
    own.start()
    everything = pltpu.make_async_remote_copy(
        src_ref=packed.at[pl.ds(0, devices - 1)],
        dst_ref=arrived.at[pl.ds(0, devices - 1)],
        send_sem=spread_sem,
        recv_sem=gather_sem,
        device_id=place((me + 1) % devices),
        device_id_type=MESH,
    )
    everything.wait()
    for term in range(3):
        settle(term, ext_b.at[pl.ds(reach, rows)], 0, 0).wait_send()
    own.wait()
    next_store.wait()
    last_store.wait()


def in_hbm(array):
    return pltpu.with_memory_space_constraint(array, pltpu.HBM)


def finish_kernel(steps, turn, next_ref, last_ref, arrived, next_out, last_out, owned, wide, sems):
    copies = [
        pltpu.make_async_copy(next_ref, next_out, sems.at[0]),
        pltpu.make_async_copy(last_ref, last_out, sems.at[1]),
    ]
    for c in copies:
        c.start()
    step = arrived.shape[0] // steps
    for i in range(steps):
        where = pl.ds(i * step, step)
        if turn:
            span = arrived.shape[1]
            wide[where, pl.ds(0, span - turn)] = arrived[where, pl.ds(turn, span - turn)].astype(wide.dtype)
            wide[where, pl.ds(span - turn, turn)] = arrived[where, pl.ds(0, turn)].astype(wide.dtype)
        else:
            wide[where] = arrived[where].astype(wide.dtype)
        c = pltpu.make_async_copy(wide.at[where], owned.at[where], sems.at[2 + i])
        c.start()
        copies.append(c)
    for c in copies:
        c.wait()


def finish(made_next, made_last, arrived, turn):
    steps = 4
    anyspec = pl.BlockSpec(memory_space=pl.ANY)
    vmem = pl.BlockSpec(memory_space=pltpu.VMEM)
    term = jax.ShapeDtypeStruct(made_next.shape, made_next.dtype)
    return pl.pallas_call(
        functools.partial(finish_kernel, steps, turn),
        out_shape=(term, term, jax.ShapeDtypeStruct(arrived.shape, jnp.float32)),
        in_specs=[anyspec, anyspec, vmem],
        out_specs=(anyspec, anyspec, anyspec),
        scratch_shapes=[
            pltpu.VMEM(arrived.shape, jnp.float32),
            pltpu.SemaphoreType.DMA((2 + steps,)),
        ],
        compiler_params=pltpu.CompilerParams(vmem_limit_bytes=16 * 1024 * 1024),
        name="finish",
    )(made_next, made_last, arrived)


def on_device(h_blocks, h_cols, t_prev, t_cur, cheb_coeffs, owner_slot):
    rows, slots, bs, _ = h_blocks.shape
    width = t_cur.shape[1]
    devices = lax.axis_size(AXES)
    reach = rows // 2
    per_dev = width // devices
    pieces = next(p for p in (6, 2) if reach % p == 0)
    group = max(1, 16 // per_dev)
    group = group if rows % group == 0 else rows
    piece = reach // pieces
    turn = pieces // 2 * piece * per_dev if piece % group == 0 else 0
    anyspec = pl.BlockSpec(memory_space=pl.ANY)
    hbm = pl.BlockSpec(memory_space=pltpu.HBM)
    dma = pltpu.SemaphoreType.DMA
    term = jax.ShapeDtypeStruct((rows, bs, width), t_cur.dtype)
    ext = pltpu.VMEM((rows + 2 * reach, bs, width), t_cur.dtype)
    near = pltpu.VMEM((rows + reach, bs, width), t_cur.dtype)
    own = pltpu.VMEM((rows, bs, width), t_cur.dtype)
    made_next, made_last, arrived = pl.pallas_call(
        functools.partial(whole_kernel, (reach, pieces, per_dev, group)),
        out_shape=(term, term, jax.ShapeDtypeStruct((devices, rows * per_dev, bs), jnp.bfloat16)),
        in_specs=[hbm] * 6,
        out_specs=(anyspec, anyspec, anyspec),
        scratch_shapes=[
            pltpu.SMEM((slots, rows), jnp.int32),
            pltpu.SMEM(cheb_coeffs.shape, cheb_coeffs.dtype),
            pltpu.VMEM((1, width), jnp.int32),
            pltpu.VMEM(h_blocks.shape, h_blocks.dtype),
            ext,
            ext,
            ext,
            near,
            near,
            own,
            own,
            pltpu.VMEM((devices, rows * per_dev, bs), jnp.bfloat16),
            pltpu.VMEM((devices * group * per_dev, bs), jnp.float32),
            pltpu.VMEM((width, width), jnp.bfloat16),
            pltpu.SMEM((rows, slots), jnp.int32),
            dma((3,)),
            dma((4,)),
            dma((3,)),
            dma((3, 2, 2)),
            dma((2,)),
            dma,
            dma,
            dma((3,)),
            pltpu.SemaphoreType.REGULAR((len(hops_of(devices)),)),
            dma((3,)),
        ],
        compiler_params=pltpu.CompilerParams(collective_id=0, has_side_effects=True, vmem_limit_bytes=46 * 1024 * 1024),
        name="whole",
    )(
        in_hbm(h_cols.T),
        in_hbm(cheb_coeffs),
        in_hbm(owner_slot[None, :]),
        h_blocks,
        in_hbm(t_prev.reshape(rows, bs, width)),
        in_hbm(t_cur.reshape(rows, bs, width)),
    )
    made_next, made_last, owned = finish(made_next, made_last, arrived, turn)
    owned = owned.reshape(devices * rows, per_dev, bs)
    owned = owned.transpose(1, 0, 2).reshape(per_dev, devices * rows * bs)
    return (made_next.reshape(-1, width), made_last.reshape(-1, width), owned)


def solution(mesh):
    return jax.shard_map(
        on_device,
        mesh=mesh,
        in_specs=(
            P(("blk", "grp"), None, None, None),
            P(("blk", "grp"), None),
            P(("blk", "grp"), None),
            P(("blk", "grp"), None),
            P(),
            P(),
        ),
        out_specs=(P(("blk", "grp"), None), P(("blk", "grp"), None), P(("blk", "grp"), None)),
        check_vma=False,
    )
```

```python
import functools

import jax
import jax.numpy as jnp
from jax import lax
from jax.experimental import pallas as pl
from jax.experimental.pallas import tpu as pltpu
from jax.sharding import PartitionSpec as P

AXES = ("blk", "grp")

MESH = pl.DeviceIdType.MESH


def hops_of(devices):
    hops, known = [], 1
    while known < devices // 2:
        hops.append(known)
        known *= 2
    return hops


def row_product(cols, row, h_ref, ext, cut):
    slots, last = h_ref.shape[1], ext.shape[0] - 1
    at = [cols[row, k] if cut == 0 else jnp.clip(cols[row, k] - cut, 0, last) for k in range(slots)]
    rhs = jnp.concatenate([ext[a] for a in at], axis=0)
    lhs = jnp.concatenate([h_ref[row, k] for k in range(slots)], axis=1)
    return jnp.dot(lhs, rhs, preferred_element_type=jnp.float32)


def whole_kernel(
    shape, h_cols_hbm, coeffs_hbm, owner_hbm, h_hbm, prev_hbm, cur_hbm, next_out, last_out, arrived,
    h_cols, coeffs, owner, h_ref, ext_a, ext_b, ext_c, near_a, near_c, prev_ref, last_ref, packed, stage, chooser, cols,
    load_sem, h_sem, send_sem, recv_sem, move_sem, spread_sem, gather_sem, out_sem, meet_sem, small_sem, go_sem,
):
    reach, pieces, per_dev, group = shape
    rows, _, bs, width = h_ref.shape[0], h_ref.shape[1], h_ref.shape[2], ext_a.shape[2]
    piece = reach // pieces
    blks, grps = lax.axis_size("blk"), lax.axis_size("grp")
    devices = blks * grps
    blk, grp = lax.axis_index("blk"), lax.axis_index("grp")
    me = blk * grps + grp

    def place(linear):
        return (linear // grps, linear % grps)

    half = pieces // 2
    inner = half * piece
    first_side = grp % 2

    def middle_first(c):
        side = (first_side + c // half) % 2
        edge = c // pieces
        return side, edge, side * reach + spot(side, edge, c % half)

    def edge_first(c):
        side = (first_side + c // pieces) % 2
        edge = 1 - (c // half) % 2
        return side, edge, side * reach + spot(side, edge, c % half)

    def spot(side, edge, j):
        return ((edge + side + 1) % 2) * inner + j * piece

    def h_load(g):
        side = (first_side + g % 2) % 2
        where = pl.ds(side * reach + spot(side, g // 2, 0), inner)
        return pltpu.make_async_copy(h_hbm.at[where], h_ref.at[where], h_sem.at[g])

    def halo(term, source, offset, full, near, where):
        side, edge, base = where
        there = (1 - 2 * side) * rows + base + reach
        if near is None:
            dest = full.at[pl.ds(there, piece)]
        else:
            dest = near.at[pl.ds(there - inner, piece)]
        return pltpu.make_async_remote_copy(
            src_ref=source.at[pl.ds(offset + base, piece)],
            dst_ref=dest,
            send_sem=send_sem.at[term],
            recv_sem=recv_sem.at[term, side, edge],
            device_id=place((me + devices - 1 + 2 * side) % devices),
            device_id_type=MESH,
        )

    def settle(term, copied, side, edge):
        return pltpu.make_async_remote_copy(
            src_ref=copied,
            dst_ref=copied,
            send_sem=send_sem.at[term],
            recv_sem=recv_sem.at[term, side, edge],
            device_id=place((me + 1) % devices),
            device_id_type=MESH,
        )

    def landed(term, edge):
        for side in range(2):
            settle(term, ext_a.at[pl.ds(0, inner)], side, edge).wait_recv()

    jump = (grp == 0) | (grp == grps - 1)

    prev_load = pltpu.make_async_copy(prev_hbm, prev_ref, load_sem.at[0])
    cur_load = pltpu.make_async_copy(cur_hbm, ext_a.at[pl.ds(reach, rows)], load_sem.at[1])
    near_load = pltpu.make_async_copy(cur_hbm, near_a.at[pl.ds(inner, rows)], load_sem.at[2])
    barrier = pltpu.get_barrier_semaphore()

    def signal_pair(semaphore, hop):
        for other in (me + hop, me + devices - hop):
            pl.semaphore_signal(semaphore, inc=1, device_id=place(other % devices), device_id_type=MESH)

    small_loads = [
        pltpu.make_async_copy(h_cols_hbm, h_cols, small_sem.at[0]),
        pltpu.make_async_copy(coeffs_hbm, coeffs, small_sem.at[1]),
        pltpu.make_async_copy(owner_hbm, owner, small_sem.at[2]),
    ]

    def loads():
        near_load.start()
        cur_load.start()
        prev_load.start()

    signal_pair(barrier, 1)
    for c in small_loads:
        c.start()
    pl.when(jump)(loads)
    pl.semaphore_wait(barrier, 2)
    start_order = [edge_first(c) for c in range(2 * pieces)]
    edges = [c for c in range(2 * pieces) if (c // half) % 2 == 0]
    outers = [c for c in range(2 * pieces) if (c // half) % 2 == 1]
    def send_edges():
        for c in edges[:half]:
            halo(0, cur_hbm, 0, ext_a, near_a, start_order[c]).start()

    pl.when(jnp.logical_not(jump))(send_edges)
    for c in edges[half:]:
        halo(0, cur_hbm, 0, ext_a, near_a, start_order[c]).start()
    pl.when(jnp.logical_not(jump))(loads)

    def send_outers():
        for c in outers[:half]:
            halo(0, cur_hbm, 0, ext_a, None, start_order[c]).start()

    pl.when(jnp.logical_not(jump))(send_outers)
    for c in outers[half:]:
        halo(0, cur_hbm, 0, ext_a, None, start_order[c]).start()
    cur_load.wait()
    near_load.wait()
    prev_load.wait()
    for g in range(2):
        h_load(g).start()
    for c in small_loads:
        c.wait()
    hops = hops_of(devices)

    ahead = list(range(len(hops) + 1))

    def meet():
        if ahead:
            step = ahead.pop(0)
            if step > 0:
                pl.semaphore_wait(meet_sem.at[step - 1], 2)
            if step < len(hops):
                signal_pair(meet_sem.at[step], hops[step])

    meet()

    q = lax.broadcasted_iota(jnp.int32, chooser.shape, 0)
    slot = (q % devices) * per_dev + q // devices
    chooser[...] = jnp.where(slot == owner[...], 1.0, 0.0).astype(chooser.dtype)

    total_rows = rows * devices

    def local_row(row, carry):
        for k in range(h_ref.shape[1]):
            at = h_cols[k, row] - me * rows + reach
            at = jnp.where(at < 0, at + total_rows, at)
            at = jnp.where(at >= total_rows, at - total_rows, at)
            cols[row, k] = jnp.clip(at, 0, rows + 2 * reach - 1)
        return carry

    lax.fori_loop(0, rows, local_row, 0)
    for g in range(2, 4):
        h_load(g).start()
    meet()

    @pl.when(jump)
    def _():
        pl.semaphore_wait(go_sem, 1)
        send_edges()
        send_outers()

    def rows_of(where, ext, cut, old, old_at, stores):
        for r in range(piece):
            row = where[2] + r
            total = row_product(cols, row, h_ref, ext, cut)
            fresh = 2.0 * total - old[old_at + row].astype(jnp.float32)
            for new, new_at in stores:
                new[new_at + row] = fresh.astype(new.dtype)

    def loop(low, high, order, ext, cut, old, old_at, stores, ready, done):
        def one_piece(c, carry):
            where = order(c)
            ready(c)
            rows_of(where, ext, cut, old, old_at, stores)
            done(c, where)
            return carry

        lax.fori_loop(low, high, one_piece, 0)

    def split_term(term, ext, near, old, old_at, stores, ready, done):
        landed(term, 1)
        moves = [
            pltpu.make_async_copy(near.at[pl.ds(0, inner)], ext.at[pl.ds(inner, inner)], move_sem.at[0]),
            pltpu.make_async_copy(
                near.at[pl.ds(inner + rows, inner)], ext.at[pl.ds(reach + rows, inner)], move_sem.at[1]
            ),
        ]
        for m in moves:
            m.start()
        loop(0, pieces, middle_first, near, inner, old, old_at, stores, ready, done)
        for m in moves:
            m.wait()
        if term == 0:
            meet()
        landed(term, 0)
        if term == 0:

            @pl.when((grp == 1) | (grp == grps - 2))
            def _():
                pl.semaphore_signal(go_sem, inc=1, device_id=place(me + 1 - 2 * (grp % 2)), device_id_type=MESH)
        loop(pieces, 2 * pieces, middle_first, ext, 0, old, old_at, stores, ready, done)

    def nothing(c):
        pass

    def h_ready(c):
        @pl.when(c % half == 0)
        def _():
            h_load(c // half).wait()

    split_term(
        0, ext_a, near_a, prev_ref, 0, [(ext_b, reach)], h_ready,
        lambda c, where: halo(1, ext_b, reach, ext_b, None, where).start(),
    )
    meet()
    landed(1, 1)
    landed(1, 0)
    both = [(ext_c, reach), (near_c, inner)]
    for part in range(4):
        to_near = near_c if part % 2 == 0 else None
        loop(
            part * half, (part + 1) * half, edge_first, ext_b, 0, ext_a, reach, both, nothing,
            lambda c, where: halo(2, ext_c, reach, ext_c, to_near, where).start(),
        )
    while ahead:
        meet()
    next_store = pltpu.make_async_copy(ext_c.at[pl.ds(reach, rows)], next_out, out_sem.at[0])
    next_store.start()

    interleaved = piece % group == 0

    def place_of(row):
        return jnp.where(row < rows - inner, row + inner, row + inner - rows) if interleaved else row

    def pack(first):
        for b in range(group):
            row = first + b
            dens = coeffs[0] * ext_b[reach + row].astype(jnp.float32)
            dens = dens + coeffs[1] * ext_c[reach + row].astype(jnp.float32)
            dens = dens + coeffs[2] * last_ref[row].astype(jnp.float32)
            turned = lax.dot_general(
                chooser[...], dens.astype(jnp.bfloat16), (((1,), (1,)), ((), ())),
                preferred_element_type=jnp.float32,
            )
            for s in range(per_dev):
                stage[pl.ds(b * per_dev + s, devices, stride=group * per_dev), :] = turned[
                    s * devices : (s + 1) * devices
                ]
        span = group * per_dev
        at = place_of(first)
        tiles = stage[...].reshape(devices, span, bs).astype(packed.dtype)
        packed[:, pl.ds(pl.multiple_of(at * per_dev, span), span), :] = tiles

    def spread(base, count):
        where = pl.ds(base * per_dev, count * per_dev)

        def one(i, carry):
            k = i // blks
            far = grps // 2
            low = (k + far - 1) % far
            high = far + (k + 3) % far
            first = jnp.where(grp < far, high, low)
            near = jnp.where(grp < far, 0, far) + (grp + 1 + k) % far
            to_blk = (blk + i + 1) % blks
            to_grp = jnp.where(k < far, first, near)
            pltpu.make_async_remote_copy(
                src_ref=packed.at[to_blk * grps + to_grp, where],
                dst_ref=arrived.at[me, where],
                send_sem=spread_sem,
                recv_sem=gather_sem,
                device_id=(to_blk, to_grp),
                device_id_type=MESH,
            ).start()
            return carry

        lax.fori_loop(0, devices - 1, one, 0)

    def last_done(c, where):
        if interleaved:
            base = where[2]

            def one_group(g, carry):
                pack(base + g * group)
                return carry

            lax.fori_loop(0, piece // group, one_group, 0)

            @pl.when(c == pieces - 1)
            def _():
                spread(reach, reach)

            @pl.when(c == 2 * pieces - 1)
            def _():
                spread(0, reach)

    split_term(2, ext_c, near_c, ext_b, reach, [(last_ref, 0)], nothing, last_done)
    last_store = pltpu.make_async_copy(last_ref, last_out, out_sem.at[1])
    last_store.start()
    if not interleaved:
        for g in range(rows // group):
            pack(g * group)
        spread(0, rows)
    own = pltpu.make_async_copy(packed.at[me], arrived.at[me], out_sem.at[2])
    own.start()
    everything = pltpu.make_async_remote_copy(
        src_ref=packed.at[pl.ds(0, devices - 1)],
        dst_ref=arrived.at[pl.ds(0, devices - 1)],
        send_sem=spread_sem,
        recv_sem=gather_sem,
        device_id=place((me + 1) % devices),
        device_id_type=MESH,
    )
    everything.wait()
    for term in range(3):
        settle(term, ext_b.at[pl.ds(reach, rows)], 0, 0).wait_send()
    own.wait()
    next_store.wait()
    last_store.wait()


def in_hbm(array):
    return pltpu.with_memory_space_constraint(array, pltpu.HBM)


def finish_kernel(steps, turn, next_ref, last_ref, arrived, next_out, last_out, owned, wide, sems):
    copies = [
        pltpu.make_async_copy(next_ref, next_out, sems.at[0]),
        pltpu.make_async_copy(last_ref, last_out, sems.at[1]),
    ]
    for c in copies:
        c.start()
    step = arrived.shape[0] // steps
    for i in range(steps):
        where = pl.ds(i * step, step)
        if turn:
            span = arrived.shape[1]
            wide[where, pl.ds(0, span - turn)] = arrived[where, pl.ds(turn, span - turn)].astype(wide.dtype)
            wide[where, pl.ds(span - turn, turn)] = arrived[where, pl.ds(0, turn)].astype(wide.dtype)
        else:
            wide[where] = arrived[where].astype(wide.dtype)
        c = pltpu.make_async_copy(wide.at[where], owned.at[where], sems.at[2 + i])
        c.start()
        copies.append(c)
    for c in copies:
        c.wait()


def finish(made_next, made_last, arrived, turn):
    steps = 4
    anyspec = pl.BlockSpec(memory_space=pl.ANY)
    vmem = pl.BlockSpec(memory_space=pltpu.VMEM)
    term = jax.ShapeDtypeStruct(made_next.shape, made_next.dtype)
    return pl.pallas_call(
        functools.partial(finish_kernel, steps, turn),
        out_shape=(term, term, jax.ShapeDtypeStruct(arrived.shape, jnp.float32)),
        in_specs=[anyspec, anyspec, vmem],
        out_specs=(anyspec, anyspec, anyspec),
        scratch_shapes=[
            pltpu.VMEM(arrived.shape, jnp.float32),
            pltpu.SemaphoreType.DMA((2 + steps,)),
        ],
        compiler_params=pltpu.CompilerParams(vmem_limit_bytes=16 * 1024 * 1024),
        name="finish",
    )(made_next, made_last, arrived)


def on_device(h_blocks, h_cols, t_prev, t_cur, cheb_coeffs, owner_slot):
    rows, slots, bs, _ = h_blocks.shape
    width = t_cur.shape[1]
    devices = lax.axis_size(AXES)
    reach = rows // 2
    per_dev = width // devices
    pieces = next(p for p in (6, 2) if reach % p == 0)
    group = max(1, 16 // per_dev)
    group = group if rows % group == 0 else rows
    piece = reach // pieces
    turn = pieces // 2 * piece * per_dev if piece % group == 0 else 0
    anyspec = pl.BlockSpec(memory_space=pl.ANY)
    hbm = pl.BlockSpec(memory_space=pltpu.HBM)
    dma = pltpu.SemaphoreType.DMA
    term = jax.ShapeDtypeStruct((rows, bs, width), t_cur.dtype)
    ext = pltpu.VMEM((rows + 2 * reach, bs, width), t_cur.dtype)
    near = pltpu.VMEM((rows + reach, bs, width), t_cur.dtype)
    own = pltpu.VMEM((rows, bs, width), t_cur.dtype)
    made_next, made_last, arrived = pl.pallas_call(
        functools.partial(whole_kernel, (reach, pieces, per_dev, group)),
        out_shape=(term, term, jax.ShapeDtypeStruct((devices, rows * per_dev, bs), jnp.bfloat16)),
        in_specs=[hbm] * 6,
        out_specs=(anyspec, anyspec, anyspec),
        scratch_shapes=[
            pltpu.SMEM((slots, rows), jnp.int32),
            pltpu.SMEM(cheb_coeffs.shape, cheb_coeffs.dtype),
            pltpu.VMEM((1, width), jnp.int32),
            pltpu.VMEM(h_blocks.shape, h_blocks.dtype),
            ext,
            ext,
            ext,
            near,
            near,
            own,
            own,
            pltpu.VMEM((devices, rows * per_dev, bs), jnp.bfloat16),
            pltpu.VMEM((devices * group * per_dev, bs), jnp.float32),
            pltpu.VMEM((width, width), jnp.bfloat16),
            pltpu.SMEM((rows, slots), jnp.int32),
            dma((3,)),
            dma((4,)),
            dma((3,)),
            dma((3, 2, 2)),
            dma((2,)),
            dma,
            dma,
            dma((3,)),
            pltpu.SemaphoreType.REGULAR((len(hops_of(devices)),)),
            dma((3,)),
            pltpu.SemaphoreType.REGULAR,
        ],
        compiler_params=pltpu.CompilerParams(collective_id=0, has_side_effects=True, vmem_limit_bytes=46 * 1024 * 1024),
        name="whole",
    )(
        in_hbm(h_cols.T),
        in_hbm(cheb_coeffs),
        in_hbm(owner_slot[None, :]),
        h_blocks,
        in_hbm(t_prev.reshape(rows, bs, width)),
        in_hbm(t_cur.reshape(rows, bs, width)),
    )
    made_next, made_last, owned = finish(made_next, made_last, arrived, turn)
    owned = owned.reshape(devices * rows, per_dev, bs)
    owned = owned.transpose(1, 0, 2).reshape(per_dev, devices * rows * bs)
    return (made_next.reshape(-1, width), made_last.reshape(-1, width), owned)


def solution(mesh):
    return jax.shard_map(
        on_device,
        mesh=mesh,
        in_specs=(
            P(("blk", "grp"), None, None, None),
            P(("blk", "grp"), None),
            P(("blk", "grp"), None),
            P(("blk", "grp"), None),
            P(),
            P(),
        ),
        out_specs=(P(("blk", "grp"), None), P(("blk", "grp"), None), P(("blk", "grp"), None)),
        check_vma=False,
    )
```

```python
import functools

import jax
import jax.numpy as jnp
from jax import lax
from jax.experimental import pallas as pl
from jax.experimental.pallas import tpu as pltpu
from jax.sharding import PartitionSpec as P

AXES = ("blk", "grp")

MESH = pl.DeviceIdType.MESH


def hops_of(devices):
    hops, known = [], 1
    while known < devices // 2:
        hops.append(known)
        known *= 2
    return hops


def row_product(cols, row, h_ref, ext, cut):
    slots, last = h_ref.shape[1], ext.shape[0] - 1
    at = [cols[row, k] if cut == 0 else jnp.clip(cols[row, k] - cut, 0, last) for k in range(slots)]
    rhs = jnp.concatenate([ext[a] for a in at], axis=0)
    lhs = jnp.concatenate([h_ref[row, k] for k in range(slots)], axis=1)
    return jnp.dot(lhs, rhs, preferred_element_type=jnp.float32)


def whole_kernel(
    shape, h_cols_hbm, coeffs_hbm, owner_hbm, h_hbm, prev_hbm, cur_hbm, next_out, last_out, arrived,
    h_cols, coeffs, owner, h_ref, ext_a, ext_b, ext_c, near_a, near_c, prev_ref, last_ref, packed, stage, chooser, cols,
    load_sem, h_sem, send_sem, recv_sem, move_sem, spread_sem, gather_sem, out_sem, meet_sem, small_sem, go_sem,
):
    reach, pieces, per_dev, group = shape
    rows, _, bs, width = h_ref.shape[0], h_ref.shape[1], h_ref.shape[2], ext_a.shape[2]
    piece = reach // pieces
    blks, grps = lax.axis_size("blk"), lax.axis_size("grp")
    devices = blks * grps
    blk, grp = lax.axis_index("blk"), lax.axis_index("grp")
    me = blk * grps + grp

    def place(linear):
        return (linear // grps, linear % grps)

    half = pieces // 2
    inner = half * piece
    first_side = grp % 2

    def middle_first(c):
        side = (first_side + c // half) % 2
        edge = c // pieces
        return side, edge, side * reach + spot(side, edge, c % half)

    def edge_first(c):
        side = (first_side + c // pieces) % 2
        edge = 1 - (c // half) % 2
        return side, edge, side * reach + spot(side, edge, c % half)

    def spot(side, edge, j):
        return ((edge + side + 1) % 2) * inner + j * piece

    def h_load(g):
        side = (first_side + g % 2) % 2
        where = pl.ds(side * reach + spot(side, g // 2, 0), inner)
        return pltpu.make_async_copy(h_hbm.at[where], h_ref.at[where], h_sem.at[g])

    def halo(term, source, offset, full, near, where):
        side, edge, base = where
        there = (1 - 2 * side) * rows + base + reach
        if near is None:
            dest = full.at[pl.ds(there, piece)]
        else:
            dest = near.at[pl.ds(there - inner, piece)]
        return pltpu.make_async_remote_copy(
            src_ref=source.at[pl.ds(offset + base, piece)],
            dst_ref=dest,
            send_sem=send_sem.at[term],
            recv_sem=recv_sem.at[term, side, edge],
            device_id=place((me + devices - 1 + 2 * side) % devices),
            device_id_type=MESH,
        )

    def settle(term, copied, side, edge):
        return pltpu.make_async_remote_copy(
            src_ref=copied,
            dst_ref=copied,
            send_sem=send_sem.at[term],
            recv_sem=recv_sem.at[term, side, edge],
            device_id=place((me + 1) % devices),
            device_id_type=MESH,
        )

    def landed(term, edge):
        for side in range(2):
            settle(term, ext_a.at[pl.ds(0, inner)], side, edge).wait_recv()

    jump = (grp == 0) | (grp == grps - 1)

    prev_load = pltpu.make_async_copy(prev_hbm, prev_ref, load_sem.at[0])
    cur_load = pltpu.make_async_copy(cur_hbm, ext_a.at[pl.ds(reach, rows)], load_sem.at[1])
    near_load = pltpu.make_async_copy(cur_hbm, near_a.at[pl.ds(inner, rows)], load_sem.at[2])
    barrier = pltpu.get_barrier_semaphore()

    def signal_pair(semaphore, hop):
        for other in (me + hop, me + devices - hop):
            pl.semaphore_signal(semaphore, inc=1, device_id=place(other % devices), device_id_type=MESH)

    small_loads = [
        pltpu.make_async_copy(h_cols_hbm, h_cols, small_sem.at[0]),
        pltpu.make_async_copy(coeffs_hbm, coeffs, small_sem.at[1]),
        pltpu.make_async_copy(owner_hbm, owner, small_sem.at[2]),
    ]

    def loads():
        near_load.start()
        cur_load.start()
        prev_load.start()

    signal_pair(barrier, 1)
    for c in small_loads:
        c.start()
    pl.when(jump)(loads)
    pl.semaphore_wait(barrier, 2)
    start_order = [edge_first(c) for c in range(2 * pieces)]
    edges = [c for c in range(2 * pieces) if (c // half) % 2 == 0]
    outers = [c for c in range(2 * pieces) if (c // half) % 2 == 1]
    def send_edges():
        for c in edges[:half]:
            halo(0, cur_hbm, 0, ext_a, near_a, start_order[c]).start()

    pl.when(jnp.logical_not(jump))(send_edges)
    for c in edges[half:]:
        halo(0, cur_hbm, 0, ext_a, near_a, start_order[c]).start()
    pl.when(jnp.logical_not(jump))(loads)

    def send_outers():
        for c in outers[:half]:
            halo(0, cur_hbm, 0, ext_a, None, start_order[c]).start()

    pl.when(jnp.logical_not(jump))(send_outers)
    for c in outers[half:]:
        halo(0, cur_hbm, 0, ext_a, None, start_order[c]).start()
    cur_load.wait()
    near_load.wait()
    prev_load.wait()
    for g in range(2):
        h_load(g).start()
    for c in small_loads:
        c.wait()
    hops = hops_of(devices)

    ahead = list(range(len(hops) + 1))

    def meet():
        if ahead:
            step = ahead.pop(0)
            if step > 0:
                pl.semaphore_wait(meet_sem.at[step - 1], 2)
            if step < len(hops):
                signal_pair(meet_sem.at[step], hops[step])

    meet()

    q = lax.broadcasted_iota(jnp.int32, chooser.shape, 0)
    slot = (q % devices) * per_dev + q // devices
    chooser[...] = jnp.where(slot == owner[...], 1.0, 0.0).astype(chooser.dtype)

    total_rows = rows * devices

    def local_row(row, carry):
        for k in range(h_ref.shape[1]):
            at = h_cols[k, row] - me * rows + reach
            at = jnp.where(at < 0, at + total_rows, at)
            at = jnp.where(at >= total_rows, at - total_rows, at)
            cols[row, k] = jnp.clip(at, 0, rows + 2 * reach - 1)
        return carry

    lax.fori_loop(0, rows, local_row, 0)
    for g in range(2, 4):
        h_load(g).start()
    meet()

    @pl.when(jump)
    def _():
        pl.semaphore_wait(go_sem, 1)
        send_edges()
        send_outers()

    def rows_of(where, ext, cut, old, old_at, stores):
        for r in range(piece):
            row = where[2] + r
            total = row_product(cols, row, h_ref, ext, cut)
            fresh = 2.0 * total - old[old_at + row].astype(jnp.float32)
            for new, new_at in stores:
                new[new_at + row] = fresh.astype(new.dtype)

    def loop(low, high, order, ext, cut, old, old_at, stores, ready, done):
        def one_piece(c, carry):
            where = order(c)
            ready(c)
            rows_of(where, ext, cut, old, old_at, stores)
            done(c, where)
            return carry

        lax.fori_loop(low, high, one_piece, 0)

    def split_term(term, ext, near, old, old_at, stores, ready, done):
        landed(term, 1)
        moves = [
            pltpu.make_async_copy(near.at[pl.ds(0, inner)], ext.at[pl.ds(inner, inner)], move_sem.at[0]),
            pltpu.make_async_copy(
                near.at[pl.ds(inner + rows, inner)], ext.at[pl.ds(reach + rows, inner)], move_sem.at[1]
            ),
        ]
        for m in moves:
            m.start()
        loop(0, half + 2, middle_first, near, inner, old, old_at, stores, ready, done)
        if term == 0:

            @pl.when((grp == 1) | (grp == grps - 2))
            def _():
                pl.semaphore_signal(go_sem, inc=1, device_id=place(me + 1 - 2 * (grp % 2)), device_id_type=MESH)
        loop(half + 2, pieces, middle_first, near, inner, old, old_at, stores, ready, done)
        for m in moves:
            m.wait()
        if term == 0:
            meet()
        landed(term, 0)
        loop(pieces, 2 * pieces, middle_first, ext, 0, old, old_at, stores, ready, done)

    def nothing(c):
        pass

    def h_ready(c):
        @pl.when(c % half == 0)
        def _():
            h_load(c // half).wait()

    split_term(
        0, ext_a, near_a, prev_ref, 0, [(ext_b, reach)], h_ready,
        lambda c, where: halo(1, ext_b, reach, ext_b, None, where).start(),
    )
    meet()
    landed(1, 1)
    landed(1, 0)
    both = [(ext_c, reach), (near_c, inner)]
    for part in range(4):
        to_near = near_c if part % 2 == 0 else None
        loop(
            part * half, (part + 1) * half, edge_first, ext_b, 0, ext_a, reach, both, nothing,
            lambda c, where: halo(2, ext_c, reach, ext_c, to_near, where).start(),
        )
    while ahead:
        meet()
    next_store = pltpu.make_async_copy(ext_c.at[pl.ds(reach, rows)], next_out, out_sem.at[0])
    next_store.start()

    interleaved = piece % group == 0

    def place_of(row):
        return jnp.where(row < rows - inner, row + inner, row + inner - rows) if interleaved else row

    def pack(first):
        for b in range(group):
            row = first + b
            dens = coeffs[0] * ext_b[reach + row].astype(jnp.float32)
            dens = dens + coeffs[1] * ext_c[reach + row].astype(jnp.float32)
            dens = dens + coeffs[2] * last_ref[row].astype(jnp.float32)
            turned = lax.dot_general(
                chooser[...], dens.astype(jnp.bfloat16), (((1,), (1,)), ((), ())),
                preferred_element_type=jnp.float32,
            )
            for s in range(per_dev):
                stage[pl.ds(b * per_dev + s, devices, stride=group * per_dev), :] = turned[
                    s * devices : (s + 1) * devices
                ]
        span = group * per_dev
        at = place_of(first)
        tiles = stage[...].reshape(devices, span, bs).astype(packed.dtype)
        packed[:, pl.ds(pl.multiple_of(at * per_dev, span), span), :] = tiles

    def spread(base, count):
        where = pl.ds(base * per_dev, count * per_dev)

        def one(i, carry):
            k = i // blks
            far = grps // 2
            low = (k + far - 1) % far
            high = far + (k + 1) % far
            first = jnp.where(grp < far, high, low)
            near = jnp.where(grp < far, 0, far) + (grp + 1 + k) % far
            to_blk = (blk + i + 1) % blks
            to_grp = jnp.where(k < far, first, near)
            pltpu.make_async_remote_copy(
                src_ref=packed.at[to_blk * grps + to_grp, where],
                dst_ref=arrived.at[me, where],
                send_sem=spread_sem,
                recv_sem=gather_sem,
                device_id=(to_blk, to_grp),
                device_id_type=MESH,
            ).start()
            return carry

        lax.fori_loop(0, devices - 1, one, 0)

    def last_done(c, where):
        if interleaved:
            base = where[2]

            def one_group(g, carry):
                pack(base + g * group)
                return carry

            lax.fori_loop(0, piece // group, one_group, 0)

            @pl.when(c == pieces - 1)
            def _():
                spread(reach, reach)

            @pl.when(c == 2 * pieces - 1)
            def _():
                spread(0, reach)

    split_term(2, ext_c, near_c, ext_b, reach, [(last_ref, 0)], nothing, last_done)
    last_store = pltpu.make_async_copy(last_ref, last_out, out_sem.at[1])
    last_store.start()
    if not interleaved:
        for g in range(rows // group):
            pack(g * group)
        spread(0, rows)
    own = pltpu.make_async_copy(packed.at[me], arrived.at[me], out_sem.at[2])
    own.start()
    everything = pltpu.make_async_remote_copy(
        src_ref=packed.at[pl.ds(0, devices - 1)],
        dst_ref=arrived.at[pl.ds(0, devices - 1)],
        send_sem=spread_sem,
        recv_sem=gather_sem,
        device_id=place((me + 1) % devices),
        device_id_type=MESH,
    )
    everything.wait()
    for term in range(3):
        settle(term, ext_b.at[pl.ds(reach, rows)], 0, 0).wait_send()
    own.wait()
    next_store.wait()
    last_store.wait()


def in_hbm(array):
    return pltpu.with_memory_space_constraint(array, pltpu.HBM)


def finish_kernel(steps, turn, next_ref, last_ref, arrived, next_out, last_out, owned, wide, sems):
    copies = [
        pltpu.make_async_copy(next_ref, next_out, sems.at[0]),
        pltpu.make_async_copy(last_ref, last_out, sems.at[1]),
    ]
    for c in copies:
        c.start()
    step = arrived.shape[0] // steps
    for i in range(steps):
        where = pl.ds(i * step, step)
        if turn:
            span = arrived.shape[1]
            wide[where, pl.ds(0, span - turn)] = arrived[where, pl.ds(turn, span - turn)].astype(wide.dtype)
            wide[where, pl.ds(span - turn, turn)] = arrived[where, pl.ds(0, turn)].astype(wide.dtype)
        else:
            wide[where] = arrived[where].astype(wide.dtype)
        c = pltpu.make_async_copy(wide.at[where], owned.at[where], sems.at[2 + i])
        c.start()
        copies.append(c)
    for c in copies:
        c.wait()


def finish(made_next, made_last, arrived, turn):
    steps = 4
    anyspec = pl.BlockSpec(memory_space=pl.ANY)
    vmem = pl.BlockSpec(memory_space=pltpu.VMEM)
    term = jax.ShapeDtypeStruct(made_next.shape, made_next.dtype)
    return pl.pallas_call(
        functools.partial(finish_kernel, steps, turn),
        out_shape=(term, term, jax.ShapeDtypeStruct(arrived.shape, jnp.float32)),
        in_specs=[anyspec, anyspec, vmem],
        out_specs=(anyspec, anyspec, anyspec),
        scratch_shapes=[
            pltpu.VMEM(arrived.shape, jnp.float32),
            pltpu.SemaphoreType.DMA((2 + steps,)),
        ],
        compiler_params=pltpu.CompilerParams(vmem_limit_bytes=16 * 1024 * 1024),
        name="finish",
    )(made_next, made_last, arrived)


def on_device(h_blocks, h_cols, t_prev, t_cur, cheb_coeffs, owner_slot):
    rows, slots, bs, _ = h_blocks.shape
    width = t_cur.shape[1]
    devices = lax.axis_size(AXES)
    reach = rows // 2
    per_dev = width // devices
    pieces = next(p for p in (6, 2) if reach % p == 0)
    group = max(1, 16 // per_dev)
    group = group if rows % group == 0 else rows
    piece = reach // pieces
    turn = pieces // 2 * piece * per_dev if piece % group == 0 else 0
    anyspec = pl.BlockSpec(memory_space=pl.ANY)
    hbm = pl.BlockSpec(memory_space=pltpu.HBM)
    dma = pltpu.SemaphoreType.DMA
    term = jax.ShapeDtypeStruct((rows, bs, width), t_cur.dtype)
    ext = pltpu.VMEM((rows + 2 * reach, bs, width), t_cur.dtype)
    near = pltpu.VMEM((rows + reach, bs, width), t_cur.dtype)
    own = pltpu.VMEM((rows, bs, width), t_cur.dtype)
    made_next, made_last, arrived = pl.pallas_call(
        functools.partial(whole_kernel, (reach, pieces, per_dev, group)),
        out_shape=(term, term, jax.ShapeDtypeStruct((devices, rows * per_dev, bs), jnp.bfloat16)),
        in_specs=[hbm] * 6,
        out_specs=(anyspec, anyspec, anyspec),
        scratch_shapes=[
            pltpu.SMEM((slots, rows), jnp.int32),
            pltpu.SMEM(cheb_coeffs.shape, cheb_coeffs.dtype),
            pltpu.VMEM((1, width), jnp.int32),
            pltpu.VMEM(h_blocks.shape, h_blocks.dtype),
            ext,
            ext,
            ext,
            near,
            near,
            own,
            own,
            pltpu.VMEM((devices, rows * per_dev, bs), jnp.bfloat16),
            pltpu.VMEM((devices * group * per_dev, bs), jnp.float32),
            pltpu.VMEM((width, width), jnp.bfloat16),
            pltpu.SMEM((rows, slots), jnp.int32),
            dma((3,)),
            dma((4,)),
            dma((3,)),
            dma((3, 2, 2)),
            dma((2,)),
            dma,
            dma,
            dma((3,)),
            pltpu.SemaphoreType.REGULAR((len(hops_of(devices)),)),
            dma((3,)),
            pltpu.SemaphoreType.REGULAR,
        ],
        compiler_params=pltpu.CompilerParams(collective_id=0, has_side_effects=True, vmem_limit_bytes=46 * 1024 * 1024),
        name="whole",
    )(
        in_hbm(h_cols.T),
        in_hbm(cheb_coeffs),
        in_hbm(owner_slot[None, :]),
        h_blocks,
        in_hbm(t_prev.reshape(rows, bs, width)),
        in_hbm(t_cur.reshape(rows, bs, width)),
    )
    made_next, made_last, owned = finish(made_next, made_last, arrived, turn)
    owned = owned.reshape(devices * rows, per_dev, bs)
    owned = owned.transpose(1, 0, 2).reshape(per_dev, devices * rows * bs)
    return (made_next.reshape(-1, width), made_last.reshape(-1, width), owned)


def solution(mesh):
    return jax.shard_map(
        on_device,
        mesh=mesh,
        in_specs=(
            P(("blk", "grp"), None, None, None),
            P(("blk", "grp"), None),
            P(("blk", "grp"), None),
            P(("blk", "grp"), None),
            P(),
            P(),
        ),
        out_specs=(P(("blk", "grp"), None), P(("blk", "grp"), None), P(("blk", "grp"), None)),
        check_vma=False,
    )
```
